128 devices in a mesh: doc: 16 (over y, z), ctx: 8 (over x, core).
Axes of the slice: x: 4, y: 4, z: 4, core: 2. Of those that a mesh axis runs over, the one named last changes fastest.
Arguments:
- tokens: bfloat16 [16, 2048, 5120], P('doc', 'ctx'), may hold values from -640 to 640
- latents: float32 [16, 512], replicated, may hold values from -6 to 6
- w_keys: bfloat16 [5120, 512], replicated, may hold values from -0.078125 to 0.078125
- w_values: bfloat16 [5120, 512], replicated, may hold values from -0.078125 to 0.078125
- w_out: bfloat16 [512, 512], replicated, may hold values from -0.25 to 0.25
- latent_gain: float32 [512], replicated, may hold values from 0.1 to 1.9
- heads_down: bfloat16 [128, 512, 5120], P(('doc', 'ctx')), may hold values from -0.25 to 0.25
- heads_up: bfloat16 [128, 512, 5120], P(('doc', 'ctx')), may hold values from -0.25 to 0.25
- owner: int32 [128], replicated, may hold values from 0 to 127, each once
- requests: bfloat16 [24576, 5120], P(('doc', 'ctx')), may hold values from -6 to 6
- req_doc: int32 [24576], P(('doc', 'ctx')), may hold values from 0 to 15
- req_module: int32 [24576, 1], P(('doc', 'ctx')), may hold values from 0 to 127; in each aligned block of 192 rows (0 to 191, 192 to 383, ...) at most 2 rows name the same one
Outputs:
- adapted: bfloat16 [24576, 5120], P(('doc', 'ctx'))
The draws below stay inside these ranges and needn't reach their ends.
Inputs may be any that keep to these rules, and one draw needn't show every extreme that they name: Module m's heads are head slot owner[m]; every slot is named once. `req_module`: the 192 request rows of one device name any one module at most 2 times, and in every draw some device names some module exactly 2 times.
All inputs are finite; a program needn't handle non-finite values.
Results may differ from the reference program's by a relative error of at most 0.012.
The reference program's roundings to bfloat16 on the way (of `key_rows`, `value_rows`, `queries`, `attended`, `summary`, `coeff` and `update`) count: a program that leaves them out, or rounds other values in their place, can miss the bound.
Values may be sent and summed in bfloat16 or wider, within the bound.
A program may use at most 128 MiB of HBM per device.

```python
import math
import jax
import jax.numpy as jnp
import numpy as np
from jax import lax

D = 5120
LAT = 16
HEADS = 4
HEAD_DIM = 128
LW = 512
REQ = 192
DOCS = 16
TOKENS = 2048
MODULES = 128
CAP = 2
N_DOC = 16
N_CTX = 8
DEVICES = 128


def draw_tokens(key, part):
    key_base = jax.random.fold_in(jax.random.fold_in(key, 17), 0)
    drawn = jnp.clip(jax.random.normal(key_base, (DOCS, TOKENS, D), jnp.float32), -4.0, 4.0)
    return drawn.astype(jnp.bfloat16)


def set_ends(entries, key, smallest, top_value):
    longest = entries.shape.index(max(entries.shape))
    spots = []
    for shift in (0, 1):
        where = [jax.random.randint(jax.random.fold_in(key, axis), (), 0, length) for axis, length in enumerate(entries.shape)]
        where[longest] = (where[longest] + shift) % entries.shape[longest]
        spots.append(tuple(where))
    return entries.at[spots[0]].set(smallest).at[spots[1]].set(top_value)


def block_scale(stream_key, shape, cuts, smallest, top_value):
    level, own = 1.0, jax.random.fold_in(stream_key, 6)
    for position, blocks in cuts:
        heights = jnp.exp(jax.random.uniform(jax.random.fold_in(own, position), (blocks,), jnp.float32, smallest / len(cuts), top_value / len(cuts)))
        level = level * jnp.repeat(heights, shape[position] // blocks).reshape([-1 if axis == position else 1 for axis in range(len(shape))])
    return level


def shared_out(own_key, own, number, rows, amount, top, bound, slope):
    order = jax.random.permutation(own_key, amount)
    crowded, usual = shares(amount, rows * top, bound, slope, True), shares(amount, rows * top, bound, slope, False)
    places = jnp.arange(amount)

    def named(sizes, turn):
        used = int((sizes > 0).sum())
        fixed = max(1, used // 4)
        passed = fixed + (places - fixed + turn * (used - fixed)) % max(1, amount - fixed)
        return jnp.zeros((amount,), jnp.int32).at[order[jnp.where(places < fixed, places, passed)]].set(jnp.asarray(sizes, jnp.int32))

    sizes = jnp.where(number % 4 == 0, named(crowded, number // 4), named(usual, number - number // 4 - 1))
    mixed = jax.random.permutation(jax.random.fold_in(own, 3), amount)
    source_of, receiver = mixed[0:amount // 2 * 2:2], mixed[1:amount // 2 * 2:2]
    margin = jnp.minimum(sizes[source_of] - 1, bound - sizes[receiver]) // 2
    margin = jnp.where((source_of == order[0]) | (receiver == order[0]) | (sizes[receiver] == 0), 0, jnp.maximum(margin, 0))
    passed = jax.random.randint(jax.random.fold_in(own, 4), (amount // 2,), 0, 1 << 20) % (margin + 1)
    sizes = sizes.at[source_of].add(-passed).at[receiver].add(passed)
    labels = jnp.searchsorted(jnp.cumsum(sizes), jnp.arange(rows * top), side="right").astype(jnp.int32)
    grid = labels.reshape(top, rows).T
    grid = grid[jax.random.permutation(jax.random.fold_in(own, 1), rows)]
    turn = jax.random.randint(jax.random.fold_in(own, 2), (rows, 1), 0, top)
    return jnp.take_along_axis(grid, (jnp.arange(top)[None, :] + turn) % top, axis=1)


def shares(number_of, total, limit, slope, full):
    loads = [(1 << 20) // math.isqrt(grade ** slope) + 1 for grade in range(1, number_of + 1)]
    largest = limit if full else min(limit, max(-(-total // number_of), total * loads[0] // sum(loads)))
    least = 1 if total - largest >= number_of - 1 else 0
    given, surplus = [largest] + [least] * (number_of - 1), total - largest - least * (number_of - 1)
    while surplus > 0:
        candidates = [i for i in range(1, number_of) if given[i] < largest] or [i for i in range(1, number_of) if given[i] < limit]
        whole, budget = sum([loads[i] for i in candidates]), surplus
        for i in candidates:
            more = min(limit - given[i], max(1, budget * loads[i] // whole), surplus)
            given[i] = given[i] + more
            surplus = surplus - more
    return np.array(given)


def bell_draw(own_key, dims, deviation, limit, pieces=(), held_as=jnp.bfloat16):
    result = jax.random.normal(own_key, dims, jnp.float32) * deviation
    if len(pieces) > 0:
        result = block_scale(own_key, dims, pieces, -0.22, 0.18) * result
    return jnp.clip(result, min=-limit, max=limit).astype(held_as)


def setup_inputs(seed: int = 0) -> dict:
    key_list = jax.random.split(jax.random.key(seed), 13)
    tokens = draw_tokens(jax.random.fold_in(key_list[12], 71), 0)
    latents = bell_draw(key_list[1], (LAT, LW), 1.0, 6.0, (), jnp.float32)
    w_keys = bell_draw(key_list[2], (D, LW), D ** -0.5, 0.078125)
    w_values = bell_draw(key_list[3], (D, LW), D ** -0.5, 0.078125)
    w_out = bell_draw(key_list[4], (LW, LW), LW ** -0.5, 0.25)
    latent_gain = jnp.clip(1.0 + 0.18 * jax.random.normal(key_list[5], (LW,), jnp.float32), 0.1, 1.9)
    heads_down = bell_draw(key_list[6], (MODULES, LW, D), LW ** -0.5, 0.25, ((0, 128),))
    heads_up = bell_draw(key_list[7], (MODULES, LW, D), LW ** -0.5, 0.25, ((0, 128),))
    owner = jax.random.permutation(key_list[8], MODULES).astype(jnp.int32)
    requests = bell_draw(key_list[9], (DEVICES * REQ, D), 1.0, 6.0, ((0, 128),))
    req_doc = set_ends(jax.random.randint(key_list[10], (DEVICES * REQ,), 0, DOCS), jax.random.fold_in(key_list[10], 1), 0, DOCS - 1).astype(jnp.int32)
    req_module_keys = jax.random.split(jax.random.fold_in(key_list[11], 1), (DEVICES * REQ) // REQ)
    req_module_turns = jax.random.permutation(jax.random.fold_in(key_list[11], 3), (DEVICES * REQ) // REQ)
    req_module = jax.vmap(lambda own, number: shared_out(jax.random.fold_in(key_list[11], 2), own, number, REQ, MODULES, 1, CAP, 2))(req_module_keys, req_module_turns).reshape((DEVICES * REQ, 1))
    return dict(tokens=tokens, latents=latents, w_keys=w_keys, w_values=w_values, w_out=w_out, latent_gain=latent_gain, heads_down=heads_down, heads_up=heads_up, owner=owner, requests=requests, req_doc=req_doc, req_module=req_module)


def apply_rows(picked_rows, tags, down_factor, up_factor):
    coeff = lax.dot_general(picked_rows, down_factor, (((1,), (1,)), ((), ())), preferred_element_type=jnp.float32) / math.sqrt(D)
    column_doc = jnp.arange(down_factor.shape[0], dtype=jnp.int32) // LAT
    matched = tags[:, None] - 1 == column_doc[None, :]
    coeff = jnp.where(matched, coeff, 0.0).astype(jnp.bfloat16)
    return (jnp.dot(coeff, up_factor, preferred_element_type=jnp.float32) / math.sqrt(LAT)).astype(jnp.bfloat16)

def reference(tokens, latents, w_keys, w_values, w_out, latent_gain, heads_down, heads_up, owner, requests, req_doc, req_module):
    flat_tokens = tokens.reshape(DOCS * TOKENS, D)
    key_rows = jnp.dot(flat_tokens, w_keys, preferred_element_type=jnp.float32).astype(jnp.bfloat16)
    value_rows = jnp.dot(flat_tokens, w_values, preferred_element_type=jnp.float32).astype(jnp.bfloat16)
    key_rows = key_rows.astype(jnp.float32).reshape(DOCS, TOKENS, HEADS, HEAD_DIM)
    value_rows = value_rows.astype(jnp.float32).reshape(DOCS, TOKENS, HEADS, HEAD_DIM)
    queries = latents.astype(jnp.bfloat16).astype(jnp.float32).reshape(LAT, HEADS, HEAD_DIM)
    scores = jnp.einsum('ihe,dthe->dhit', queries, key_rows, precision=lax.Precision.HIGHEST) / math.sqrt(HEAD_DIM)
    probs = jax.nn.softmax(scores, axis=-1)
    attended = jnp.einsum('dhit,dthe->dihe', probs, value_rows, precision=lax.Precision.HIGHEST)
    attended = attended.reshape(DOCS * LAT, LW).astype(jnp.bfloat16)
    mixed_state = latents.reshape(1, LAT, LW) + jnp.dot(attended, w_out, preferred_element_type=jnp.float32).reshape(DOCS, LAT, LW)
    summary = mixed_state * lax.rsqrt(lax.optimization_barrier(jnp.mean(mixed_state * mixed_state, axis=-1, keepdims=True)) + 1e-06) * latent_gain
    summary = summary.astype(jnp.bfloat16).reshape(DOCS * LAT, LW)
    devices = N_DOC * N_CTX
    blocks = req_module[:, 0].reshape(devices, REQ)
    block_docs = req_doc.reshape(devices, REQ)

    def per_module(module, total):
        slot = owner[module]
        down_factor = jnp.dot(summary, heads_down[slot], preferred_element_type=jnp.float32).astype(jnp.bfloat16)
        up_factor = jnp.dot(summary, heads_up[slot], preferred_element_type=jnp.float32).astype(jnp.bfloat16)
        order = jnp.argsort(jnp.where(blocks == module, 0, 1), axis=1, stable=True)[:, :CAP].astype(jnp.int32)
        picked = jnp.take_along_axis(blocks, order, axis=1)
        valid = (picked == module).reshape(-1)
        global_rows = (jnp.arange(devices, dtype=jnp.int32)[:, None] * REQ + order).reshape(-1)
        tags = jnp.where(valid, jnp.take_along_axis(block_docs, order, axis=1).reshape(-1) + 1, 0)
        update = apply_rows(requests[global_rows], tags, down_factor, up_factor)
        return total.at[global_rows].add(jnp.where(valid[:, None], update.astype(jnp.float32), 0.0))
    total = lax.fori_loop(0, MODULES, per_module, jnp.zeros((devices * REQ, D), jnp.float32))
    return (requests.astype(jnp.float32) + total).astype(jnp.bfloat16)
```

```python
import functools
import math

import jax
import jax.numpy as jnp
from jax import lax
from jax.experimental import pallas as pl
from jax.experimental.pallas import tpu as pltpu
from jax.sharding import PartitionSpec as P

MESH = pl.DeviceIdType.MESH
BF = jnp.bfloat16
F32 = jnp.float32

D = 5120
LAT = 16
HEADS = 4
LW = 512
REQ = 192
ND = 16
NC = 8
DEV = ND * NC
ROWS = 2 * DEV
BC = 2 * ND
BD = 2 * NC
C = 8
W = D // C


def iota(shape, dim):
    return lax.broadcasted_iota(jnp.int32, shape, dim)


def to_column(row, n):
    m = row.shape[1]
    spread = jnp.broadcast_to(row, (n, m))
    return jnp.sum(
        jnp.where(iota((n, m), 0) == iota((n, m), 1), spread, jnp.zeros_like(spread)),
        axis=1,
        keepdims=True,
    )


def to_row(column, m):
    n = column.shape[0]
    spread = jnp.broadcast_to(column, (n, m))
    return jnp.sum(
        jnp.where(iota((n, m), 0) == iota((n, m), 1), spread, jnp.zeros_like(spread)),
        axis=0,
        keepdims=True,
    )


def kernel(
    tok_h, lat_h, wk_h, wv_h, wo_h, gain_h, hd_h, hu_h, own_h, req_h, doc_h, mod_h,
    out_h,
    tok, wk, wv, wo, lat, gain, hd, hu, own, req, rdoc, rmod,
    acc_k, acc_v, cx, sm, down, up, coeff_acc, coeff_b,
    placer, placer_t, perm, perm_back,
    tag_s1, tag_r1, tag_s2, tag_r2,
    s1, r1, s2, r2, s3, r3, s4, r4, outb,
    ld_small, ld_req, ld_tok, ld_head, st_out,
    ss1, rs1, ss2, rs2, ss3, rs3, ss4, rs4,
    sst, rst, ssx, rsx, ssd, rsd,
):
    me_d = lax.axis_index("doc")
    me_c = lax.axis_index("ctx")

    def ctx_peer(k):
        return lax.rem(me_c + k, NC)

    def doc_peer(k):
        y = lax.rem(me_d // 4 + k // 4, 4)
        z = lax.rem(lax.rem(me_d, 4) + lax.rem(k, 4), 4)
        return y * 4 + z

    small = [
        (own_h, own), (doc_h, rdoc), (mod_h, rmod), (lat_h, lat), (gain_h, gain), (wo_h, wo),
    ]
    small_copies = [
        pltpu.make_async_copy(a, b, ld_small.at[i]) for i, (a, b) in enumerate(small)
    ]
    for cp in small_copies[:3]:
        cp.start()

    def cols(c):
        return pl.ds(pl.multiple_of(c * W, 128), W)

    def req_copy(c):
        return pltpu.make_async_copy(req_h.at[:, cols(c)], req.at[c], ld_req.at[c])

    def tok_copies(c):
        rows = pl.ds(pl.multiple_of(c * W, 128), W)
        return (
            pltpu.make_async_copy(tok_h.at[0, :, cols(c)], tok.at[c], ld_tok.at[0, c]),
            pltpu.make_async_copy(wk_h.at[rows], wk.at[c], ld_tok.at[1, c]),
            pltpu.make_async_copy(wv_h.at[rows], wv.at[c], ld_tok.at[2, c]),
        )

    def head_copies(c):
        return (
            pltpu.make_async_copy(hd_h.at[0, :, cols(c)], hd.at[c], ld_head.at[0, c]),
            pltpu.make_async_copy(hu_h.at[0, :, cols(c)], hu.at[c], ld_head.at[1, c]),
        )

    def out_copy(c):
        return pltpu.make_async_copy(outb.at[c], out_h.at[:, cols(c)], st_out.at[c])

    def each(n, body, start=0):
        def step(k, carry):
            body(k)
            return carry

        lax.fori_loop(start, n, step, 0)

    barrier = pltpu.get_barrier_semaphore()
    each(NC, lambda k: pl.semaphore_signal(
        barrier, inc=1, device_id={"ctx": ctx_peer(k)}, device_id_type=MESH), 1)
    each(ND, lambda k: pl.semaphore_signal(
        barrier, inc=1, device_id={"doc": doc_peer(k)}, device_id_type=MESH), 1)

    each(C, lambda c: req_copy(c).start())

    def start_tok(c):
        for cp in tok_copies(c):
            cp.start()

    def start_heads(c):
        for cp in head_copies(c):
            cp.start()

    each(C, start_tok)
    for cp in small_copies[3:]:
        cp.start()
    each(C, start_heads)

    for cp in small_copies[:3]:
        cp.wait()
    mod_row = rmod[...]
    mod_col = to_column(mod_row.astype(F32), REQ).astype(jnp.int32)
    own_col = to_column(own[...].astype(F32), DEV)
    picked = iota((DEV, REQ), 0) == mod_row
    target = jnp.sum(jnp.where(picked, own_col, 0.0), axis=0, keepdims=True).astype(jnp.int32)
    earlier = (mod_col == mod_row) & (iota((REQ, REQ), 0) < iota((REQ, REQ), 1))
    rank = jnp.sum(jnp.where(earlier, 1.0, 0.0), axis=0, keepdims=True).astype(jnp.int32)
    spot = lax.rem(target, NC) * BC + (target // NC) * 2 + rank
    spot_col = to_column(spot.astype(F32), REQ).astype(jnp.int32)
    tag_col = to_column((rdoc[...] + 1).astype(F32), REQ)
    placer[...] = jnp.where(iota((ROWS, REQ), 0) == spot, 1.0, 0.0).astype(BF)
    placer_t[...] = jnp.where(iota((REQ, ROWS), 1) == spot_col, 1.0, 0.0).astype(BF)
    i = iota((ROWS, ROWS), 0)
    j = iota((ROWS, ROWS), 1)
    there = ((i >> 1) & 7) * BC + (i >> 4) * 2 + (i & 1)
    perm[...] = jnp.where(j == there, 1.0, 0.0).astype(BF)
    back = ((i >> 1) & 15) * BD + (i >> 5) * 2 + (i & 1)
    perm_back[...] = jnp.where(j == back, 1.0, 0.0).astype(BF)
    tag_s1[...] = jnp.dot(
        placer[...], jnp.broadcast_to(tag_col, (REQ, 128)).astype(BF), preferred_element_type=F32
    ).astype(BF)

    own_c = pl.ds(pl.multiple_of(me_c * BC, BC), BC)
    own_d = pl.ds(pl.multiple_of(me_d * BD, BD), BD)

    def to_ctx(src, dst, ssem, rsem):
        def send(k):
            p = ctx_peer(k)
            pltpu.make_async_remote_copy(
                src_ref=src.at[pl.ds(pl.multiple_of(p * BC, BC), BC)],
                dst_ref=dst.at[own_c],
                send_sem=ssem, recv_sem=rsem,
                device_id={"ctx": p}, device_id_type=MESH,
            ).start()

        each(NC, send, 1)
        dst[own_c, :] = src[own_c, :]

    def to_doc(src, dst, ssem, rsem):
        def send(k):
            p = doc_peer(k)
            pltpu.make_async_remote_copy(
                src_ref=src.at[pl.ds(pl.multiple_of(p * BD, BD), BD)],
                dst_ref=dst.at[own_d],
                send_sem=ssem, recv_sem=rsem,
                device_id={"doc": p}, device_id_type=MESH,
            ).start()

        each(ND, send, 1)
        dst[own_d, :] = src[own_d, :]

    def await_rows(buf, sem, n):
        part = buf.at[pl.ds(0, n)]
        pltpu.make_async_copy(part, part, sem).wait()

    NB = (NC - 1) * BC
    NA = (ND - 1) * BD

    pl.semaphore_wait(barrier, NC + ND - 2)
    to_ctx(tag_s1, tag_r1, sst.at[0], rst.at[0])

    def pack(c):
        req_copy(c).wait()
        s1[c] = jnp.dot(placer[...], req[c], preferred_element_type=F32).astype(BF)
        to_ctx(s1.at[c], r1.at[c], ss1.at[c], rs1.at[c])

    def relay(c):
        await_rows(r1.at[c], rs1.at[c], NB)
        s2[c] = jnp.dot(perm[...], r1[c], preferred_element_type=F32).astype(BF)
        to_doc(s2.at[c], r2.at[c], ss2.at[c], rs2.at[c])

    def project(c):
        for cp in tok_copies(c):
            cp.wait()
        acc_k[...] += jnp.dot(tok[c], wk[c], preferred_element_type=F32)
        acc_v[...] += jnp.dot(tok[c], wv[c], preferred_element_type=F32)

    def attend():
        for cp in small_copies[3:]:
            cp.wait()
        queries = lat[...].astype(BF)
        keys = acc_k[...].astype(BF)
        values = acc_v[...].astype(BF).astype(F32)
        peaks, totals = [], []
        for h in range(HEADS):
            part = slice(128 * h, 128 * (h + 1))
            scores = lax.dot_general(
                queries[:, part], keys[:, part], (((1,), (1,)), ((), ())),
                preferred_element_type=F32,
            ) / math.sqrt(128)
            peak = jnp.max(scores, axis=1, keepdims=True)
            expo = jnp.exp(scores - peak)
            peaks.append(peak)
            totals.append(jnp.sum(expo, axis=1, keepdims=True))
            cx[me_c, LAT * h : LAT * (h + 1), :] = jnp.dot(
                expo, values[:, part], precision=lax.Precision.HIGHEST,
                preferred_element_type=F32,
            )
        peak_row = to_row(jnp.concatenate(peaks, axis=0), 128)
        total_row = to_row(jnp.concatenate(totals, axis=0), 128)
        line = iota((8, 128), 0)
        cx[me_c, HEADS * LAT :, :] = jnp.where(
            line == 0, peak_row, jnp.where(line == 1, total_row, 0.0)
        )

        def send(k):
            pltpu.make_async_remote_copy(
                src_ref=cx.at[me_c], dst_ref=cx.at[me_c],
                send_sem=ssx.at[0], recv_sem=rsx.at[0],
                device_id={"ctx": ctx_peer(k)}, device_id_type=MESH,
            ).start()

        each(NC, send, 1)

    def summarize():
        part = cx.at[pl.ds(0, NC - 1)]
        pltpu.make_async_copy(part, part, rsx.at[0]).wait()
        n = HEADS * LAT
        peaks = [to_column(cx[k, n : n + 1, :], n) for k in range(NC)]
        totals = [to_column(cx[k, n + 1 : n + 2, :], n) for k in range(NC)]
        top = functools.reduce(jnp.maximum, peaks)
        ratios = [jnp.exp(p - top) for p in peaks]
        total = functools.reduce(jnp.add, [t * r for t, r in zip(totals, ratios)])
        weighted = functools.reduce(
            jnp.add, [cx[k, :n, :] * ratios[k] for k in range(NC)]
        ) / total
        attended = jnp.concatenate(
            [weighted[LAT * h : LAT * (h + 1)] for h in range(HEADS)], axis=1
        ).astype(BF)
        mixed = lat[...] + jnp.dot(attended, wo[...], preferred_element_type=F32)
        summary = (
            mixed
            * lax.rsqrt(jnp.mean(mixed * mixed, axis=-1, keepdims=True) + 1e-06)
            * gain[...]
        )
        sm[me_d] = summary.astype(BF)

        def send(k):
            pltpu.make_async_remote_copy(
                src_ref=sm.at[me_d], dst_ref=sm.at[me_d],
                send_sem=ssd.at[0], recv_sem=rsd.at[0],
                device_id={"doc": doc_peer(k)}, device_id_type=MESH,
            ).start()

        each(ND, send, 1)

    def await_summaries():
        part = sm.at[pl.ds(0, ND - 1)]
        pltpu.make_async_copy(part, part, rsd.at[0]).wait()

    def factors(c):
        for cp in head_copies(c):
            cp.wait()
        summaries = sm[...].reshape(ND * LAT, LW)
        down[c] = jnp.dot(summaries, hd[c], preferred_element_type=F32).astype(BF)
        up[c] = jnp.dot(summaries, hu[c], preferred_element_type=F32).astype(BF)

    def coefficients(c):
        await_rows(r2.at[c], rs2.at[c], NA)
        coeff_acc[...] += lax.dot_general(
            r2[c], down[c], (((1,), (1,)), ((), ())), preferred_element_type=F32
        )

    acc_k[...] = jnp.zeros_like(acc_k)
    acc_v[...] = jnp.zeros_like(acc_v)
    coeff_acc[...] = jnp.zeros_like(coeff_acc)
    each(2, pack)
    each(C // 2, project)

    await_rows(tag_r1, rst.at[0], NB)
    tag_s2[...] = jnp.dot(perm[...], tag_r1[...], preferred_element_type=F32).astype(BF)
    to_doc(tag_s2, tag_r2, sst.at[1], rst.at[1])

    def tick(t):
        relay(t)

        @pl.when(t + 2 < C)
        def _():
            pack(t + 2)

        @pl.when(t == 0)
        def _():
            each(C, project, C // 2)
            attend()

        @pl.when(t == 2)
        def _():
            summarize()

        @pl.when(t == 4)
        def _():
            await_summaries()

        @pl.when((t == 4) | (t == 5))
        def _():
            def pair(k):
                factors((t - 4) * (C // 2) + k)
            each(C // 2, pair)

        @pl.when((t == 6) | (t == 7))
        def _():
            def some(k):
                coefficients((t - 6) * 3 + k)
            each(3, some)

    each(C, tick)
    each(C, coefficients, 6)

    await_rows(tag_r2, rst.at[1], NA)
    tags = tag_r2[...].astype(F32)
    column_tag = (iota((ROWS, 2 * 128), 1) // LAT + 1).astype(F32)
    matched = jnp.concatenate([tags, tags], axis=1) == column_tag
    coeff_b[...] = jnp.where(matched, coeff_acc[...] / math.sqrt(D), 0.0).astype(BF)

    def update(c):
        s3[c] = (
            jnp.dot(coeff_b[...], up[c], preferred_element_type=F32) / math.sqrt(LAT)
        ).astype(BF)
        to_doc(s3.at[c], r3.at[c], ss3.at[c], rs3.at[c])

    def relay_back(c):
        await_rows(r3.at[c], rs3.at[c], NA)
        s4[c] = jnp.dot(perm_back[...], r3[c], preferred_element_type=F32).astype(BF)
        to_ctx(s4.at[c], r4.at[c], ss4.at[c], rs4.at[c])

    def finish(c):
        await_rows(r4.at[c], rs4.at[c], NB)
        gathered = jnp.dot(placer_t[...], r4[c], preferred_element_type=F32)
        outb[c] = (req[c].astype(F32) + gathered).astype(BF)
        out_copy(c).start()

    each(C, update)

    def tock(t):
        @pl.when(t < C)
        def _():
            relay_back(t)

        @pl.when(t > 0)
        def _():
            finish(t - 1)

    each(C + 1, tock)

    def drain(c):
        await_rows(s1.at[c], ss1.at[c], NB)
        await_rows(s2.at[c], ss2.at[c], NA)
        await_rows(s3.at[c], ss3.at[c], NA)
        await_rows(s4.at[c], ss4.at[c], NB)
        out_copy(c).wait()

    await_rows(tag_s1, sst.at[0], NB)
    await_rows(tag_s2, sst.at[1], NA)
    part = cx.at[pl.ds(0, NC - 1)]
    pltpu.make_async_copy(part, part, ssx.at[0]).wait()
    part = sm.at[pl.ds(0, ND - 1)]
    pltpu.make_async_copy(part, part, ssd.at[0]).wait()
    each(C, drain)


def on_device(
    tokens, latents, w_keys, w_values, w_out, latent_gain, heads_down, heads_up,
    owner, requests, req_doc, req_module,
):
    vm = pltpu.VMEM
    dma = pltpu.SemaphoreType.DMA
    slab = vm((C, ROWS, W), BF)
    scratch = [
        vm((C, 256, W), BF), vm((C, W, LW), BF), vm((C, W, LW), BF), vm((LW, LW), BF),
        vm((LAT, LW), F32), vm((1, LW), F32),
        vm((C, LW, W), BF), vm((C, LW, W), BF),
        vm((1, DEV), jnp.int32), vm((C, REQ, W), BF), vm((1, REQ), jnp.int32),
        vm((1, REQ), jnp.int32),
        vm((256, LW), F32), vm((256, LW), F32),
        vm((NC, HEADS * LAT + 8, 128), F32), vm((ND, LAT, LW), BF),
        slab, slab, vm((ROWS, ROWS), F32), vm((ROWS, ROWS), BF),
        vm((ROWS, REQ), BF), vm((REQ, ROWS), BF), vm((ROWS, ROWS), BF), vm((ROWS, ROWS), BF),
        vm((ROWS, 128), BF), vm((ROWS, 128), BF), vm((ROWS, 128), BF), vm((ROWS, 128), BF),
        slab, slab, slab, slab, slab, slab, slab, slab, vm((C, REQ, W), BF),
        dma((6,)), dma((C,)), dma((3, C)), dma((2, C)), dma((C,)),
        dma((C,)), dma((C,)), dma((C,)), dma((C,)), dma((C,)), dma((C,)), dma((C,)), dma((C,)),
        dma((2,)), dma((2,)), dma((1,)), dma((1,)), dma((1,)), dma((1,)),
    ]
    hbm = pl.BlockSpec(memory_space=pl.ANY)
    return pl.pallas_call(
        kernel,
        out_shape=jax.ShapeDtypeStruct((REQ, D), BF),
        in_specs=[hbm] * 12,
        out_specs=hbm,
        scratch_shapes=scratch,
        compiler_params=pltpu.CompilerParams(
            collective_id=0, has_side_effects=True, vmem_limit_bytes=64 * 1024 * 1024 - 131072
        ),
    )(
        tokens, latents, w_keys, w_values, w_out, latent_gain.reshape(1, LW), heads_down,
        heads_up, owner.reshape(1, DEV), requests, req_doc.reshape(1, REQ),
        req_module.reshape(1, REQ),
    )


def solution(mesh):
    in_specs = (
        P("doc", "ctx", None), P(), P(), P(), P(), P(),
        P(("doc", "ctx"), None, None), P(("doc", "ctx"), None, None), P(),
        P(("doc", "ctx"), None), P(("doc", "ctx")), P(("doc", "ctx"), None),
    )
    return jax.shard_map(
        on_device, mesh=mesh, in_specs=in_specs, out_specs=P(("doc", "ctx"), None),
        check_vma=False,
    )
```
